32 devices in a mesh: gx: 8 (over z, core), gy: 4 (over y, x).
Axes of the slice: x: 2, y: 2, z: 4, core: 2. Of those that a mesh axis runs over, the one named last changes fastest.
Arguments:
- offsets: float32 [384, 3, 128], P(('gx', 'gy')), may hold values from 0 to 1
- widths: float32 [384, 128], P(('gx', 'gy')), may hold values from 0.6 to 2.5
- solvation: float32 [384, 128], P(('gx', 'gy')), may hold values from -6 to 6
- heading: int32 [384, 1], P(('gx', 'gy')), may hold values from 0 to 8; in each aligned block of 12 rows (0 to 11, 12 to 23, ...) at most 3 rows name the same one
- old_map: float32 [64, 96, 1024], P('gx', 'gy'), may hold values from -6 to 6
Outputs:
- new_map: float32 [64, 96, 1024], P('gx', 'gy')
The draws below stay inside these ranges and needn't reach their ends.
Inputs may be any that keep to these rules, and one draw needn't show every extreme that they name: `heading`: entry d moves a block d // 3 - 1 tiles along x and d % 3 - 1 tiles along y from the tile of the device that stores it; among the 12 blocks of one device at most 3 share an entry.
All inputs are finite; a program needn't handle non-finite values.
Results may differ from the reference program's by a relative error of at most 0.0003.
Values sent between devices are 32-bit elements; how exact they have to be, the bound alone decides.
A program may use at most 64 MiB of HBM per device.

```python
import math
import jax
import jax.numpy as jnp
import numpy as np
from jax import lax

TX = 8
TY = 24
NZ = 1024
B_DEV = 12
ATOM_BLOCK = 128
SLOTS = 3
W = 5
NX = 64
NY = 96
NBLK = 384
N_GX = 8
N_GY = 4


def level_of(rng, dims, cuts, least, largest):
    def one(position, parts):
        draws = jax.random.uniform(jax.random.fold_in(jax.random.fold_in(rng, 6), position), (parts,), jnp.float32, least / len(cuts), largest / len(cuts))
        return jnp.repeat(jnp.exp(draws), dims[position] // parts).reshape((-1,) + (1,) * (len(dims) - position - 1))

    gain = one(*cuts[0])
    for cut in cuts[1:]:
        gain = gain * one(*cut)
    return gain


def shared_out(rng, own, number, rows, number_of, top, most, lean):
    ranking = jax.random.permutation(rng, number_of)
    heavy_load, usual = portions_of(number_of, rows * top, most, lean, True), portions_of(number_of, rows * top, most, lean, False)
    places = jnp.arange(number_of)

    def named(lengths, rotation):
        used = int((lengths > 0).sum())
        fixed = max(1, used // 4)
        passed = fixed + (places - fixed + rotation * (used - fixed)) % max(1, number_of - fixed)
        return jnp.zeros((number_of,), jnp.int32).at[ranking[jnp.where(places < fixed, places, passed)]].set(jnp.asarray(lengths, jnp.int32))

    lengths = jnp.where(number % 4 == 0, named(heavy_load, number // 4), named(usual, number - number // 4 - 1))
    mixed = jax.random.permutation(jax.random.fold_in(own, 3), number_of)
    donor, sink = mixed[0:number_of // 2 * 2:2], mixed[1:number_of // 2 * 2:2]
    margin = jnp.minimum(lengths[donor] - 1, most - lengths[sink]) // 2
    margin = jnp.where((donor == ranking[0]) | (sink == ranking[0]) | (lengths[sink] == 0), 0, jnp.maximum(margin, 0))
    passed = jax.random.randint(jax.random.fold_in(own, 4), (number_of // 2,), 0, 1 << 20) % (margin + 1)
    lengths = lengths.at[donor].add(-passed).at[sink].add(passed)
    members = jnp.searchsorted(jnp.cumsum(lengths), jnp.arange(rows * top), side="right").astype(jnp.int32)
    listing = members.reshape(top, rows).T
    listing = listing[jax.random.permutation(jax.random.fold_in(own, 1), rows)]
    rotation = jax.random.randint(jax.random.fold_in(own, 2), (rows, 1), 0, top)
    return jnp.take_along_axis(listing, (jnp.arange(top)[None, :] + rotation) % top, axis=1)


def portions_of(count, total, bound, skew, full):
    loads = [(1 << 20) // math.isqrt(rank ** skew) + 1 for rank in range(1, count + 1)]
    largest = bound if full else min(bound, max(-(-total // count), total * loads[0] // sum(loads)))
    least = 1 if total - largest >= count - 1 else 0
    given, rest = [largest] + [least] * (count - 1), total - largest - least * (count - 1)
    while rest > 0:
        movable = [i for i in range(1, count) if given[i] < largest] or [i for i in range(1, count) if given[i] < bound]
        pool, budget = sum([loads[i] for i in movable]), rest
        for i in movable:
            addition = min(bound - given[i], max(1, budget * loads[i] // pool), rest)
            given[i] = given[i] + addition
            rest = rest - addition
    return np.array(given)


def gaussian(stream_key, dims, spread, bound, split=(), held_as=jnp.bfloat16):
    gain = level_of(stream_key, dims, split, -0.22, 0.18) if split else 1.0
    values = jax.random.normal(stream_key, dims, jnp.float32) * spread * gain
    return jnp.minimum(jnp.maximum(values, -bound), bound).astype(held_as)


def setup_inputs(seed: int = 0) -> dict:
    seeds = jax.random.split(jax.random.key(seed), 6)
    offsets = jnp.clip(1.0 * jax.random.uniform(seeds[0], (NBLK, 3, ATOM_BLOCK), jnp.float32) ** level_of(seeds[0], (NBLK, 3, ATOM_BLOCK), ((0, 32),), -0.2, 0.2), 0.0, 1.0)
    widths = jnp.clip(jnp.exp(math.log(2.5) - 1.4271163 * jax.random.uniform(seeds[1], (NBLK, ATOM_BLOCK), jnp.float32) ** level_of(seeds[1], (NBLK, ATOM_BLOCK), ((0, 32),), -0.2, 0.2)), 0.6, 2.5)
    solvation = gaussian(seeds[2], (NBLK, ATOM_BLOCK), 1.0, 6.0, ((0, 32),), jnp.float32)
    heading_keys = jax.random.split(jax.random.fold_in(seeds[3], 1), NBLK // B_DEV)
    heading_turns = jax.random.permutation(jax.random.fold_in(seeds[3], 3), NBLK // B_DEV)
    heading = jax.vmap(lambda own, number: shared_out(jax.random.fold_in(seeds[3], 2), own, number, B_DEV, 9, 1, SLOTS, 2))(heading_keys, heading_turns).reshape((NBLK, 1))
    old_map = gaussian(seeds[4], (NX, NY, NZ), 1.0, 6.0, ((0, 8), (1, 4)), jnp.float32)
    return dict(offsets=offsets, widths=widths, solvation=solvation, heading=heading, old_map=old_map)


def block_field(rel, width_row, weight_row, span_x, span_y, span_z):
    alpha = 0.5 / (width_row * width_row)
    delta_x = span_x[None, :] - rel[0][:, None]
    delta_y = span_y[None, :] - rel[1][:, None]
    delta_z = span_z[None, :] - rel[2][:, None]
    along_x = jnp.exp(-alpha[:, None] * delta_x * delta_x)
    along_y = jnp.exp(-alpha[:, None] * delta_y * delta_y)
    along_z = jnp.exp(-alpha[:, None] * delta_z * delta_z)
    plane = weight_row[:, None, None] * along_x[:, :, None] * along_y[:, None, :]
    plane = plane.reshape(plane.shape[0], -1)
    return lax.dot_general(plane, along_z, (((0,), (0,)), ((), ())), precision=lax.Precision.HIGHEST)


def reference(offsets, widths, solvation, heading, old_map):
    ext_x = TX + 2 * W
    ext_y = TY + 2 * W
    span_x = jnp.arange(ext_x).astype(jnp.float32) - W
    span_y = jnp.arange(ext_y).astype(jnp.float32) - W
    span_z = jnp.arange(NZ).astype(jnp.float32)
    grid = jnp.zeros((NX + 2 * W, NY + 2 * W, NZ), jnp.float32)
    count = offsets.shape[0]

    def step(total, inputs):
        place, width_row, weight_row, target, number = inputs
        device = number // B_DEV
        tile_row = device // N_GY + target // 3 - 1
        tile_col = device % N_GY + target % 3 - 1
        inside = (tile_row >= 0) & (tile_row < N_GX) & (tile_col >= 0) & (tile_col < N_GY)
        weight_row = jnp.where(inside, weight_row, jnp.zeros_like(weight_row))
        rel = (place[0] * TX, place[1] * TY, place[2] * NZ)
        field = block_field(rel, width_row, weight_row, span_x, span_y, span_z).reshape(ext_x, ext_y, NZ)
        start_x = (jnp.clip(tile_row, 0, N_GX - 1) * TX).astype(jnp.int32)
        start_y = (jnp.clip(tile_col, 0, N_GY - 1) * TY).astype(jnp.int32)
        start_z = jnp.zeros((), jnp.int32)
        window = lax.dynamic_slice(total, (start_x, start_y, start_z), (ext_x, ext_y, NZ))
        total = lax.dynamic_update_slice(total, window + field, (start_x, start_y, start_z))
        return total, None

    numbers = jnp.arange(count).astype(jnp.int32)
    grid, unused = lax.scan(step, grid, (offsets, widths, solvation, heading[:, 0], numbers))
    return old_map + grid[W:W + NX, W:W + NY, :]
```

```python
import functools
import math

import jax
import jax.numpy as jnp
from jax import lax
from jax.experimental import pallas as pl
from jax.experimental.pallas import tpu as pltpu
from jax.sharding import PartitionSpec as P

SLOTS = 3
W = 5
ROWS = 8
HOMES = (1, 0, 1, -1, 0, 1, -1, 0, -1)
ZTILE = 256
MESH = pl.DeviceIdType.MESH
VMEM = pl.BlockSpec(memory_space=pltpu.VMEM)
SMEM = pl.BlockSpec(memory_space=pltpu.SMEM)


def pack_kernel(heading, offsets, widths, solvation, packed, taken):
    packed[...] = jnp.zeros_like(packed)
    for number in range(9):
        taken[number] = 0
    lanes = offsets.shape[2]
    filled = jnp.ones((1, lanes), jnp.float32)
    rest = jnp.zeros((2, lanes), jnp.float32)
    for block in range(offsets.shape[0]):
        target = heading[block, 0]
        rank = taken[target]
        taken[target] = rank + 1
        slot = (lax.rem(target, 3) * 3 + lax.div(target, 3)) * SLOTS + rank
        packed[slot] = jnp.concatenate(
            [offsets[block], widths[pl.ds(block, 1)], solvation[pl.ds(block, 1)], filled, rest], axis=0
        )


def split(value):
    high = value.astype(jnp.bfloat16)
    return high, (value - high.astype(jnp.float32)).astype(jnp.bfloat16)


def field_kernel(rows, blocks, core, low_edge, high_edge, total, filled, slots, homes, sem):
    tile_x, tile_y, depth = core.shape
    lanes = blocks.shape[2]
    ext_y = tile_y + 2 * W
    fetch = pltpu.make_async_copy(blocks.at[:, 5], filled, sem)
    fetch.start()
    total[...] = jnp.zeros_like(total)
    fetch.wait()
    row = lax.axis_index("gx")
    per_home = filled.shape[0] // len(HOMES)
    count = jnp.int32(0)
    for group, home in enumerate(HOMES):
        within = ((row + home >= 0) & (row + home < rows)).astype(jnp.int32)
        for place in range(per_home):
            slot = group * per_home + place
            slots[count] = slot
            homes[count] = home
            count = count + within * filled[slot, 0].astype(jnp.int32)
    slots[count] = 0
    homes[count] = 0
    root = math.sqrt(0.5 * math.log2(math.e))
    row_x = lax.broadcasted_iota(jnp.int32, (tile_x, lanes), 0)

    def factors(number):
        live = jnp.where(number < count, 1.0, 0.0)
        block = blocks[slots[number]]
        home = homes[number]
        width = jnp.where(number < count, block[3:4], 1.0)
        scale = root / width
        pz = block[2:3] * depth
        columns = jnp.concatenate([scale, pz, block[2:8]], axis=0).T
        x0 = home * tile_x
        delta_x = (row_x - x0).astype(jnp.float32) - block[0:1] * tile_x
        tx = delta_x * scale
        exp_x = -(tx * tx)
        inside = (row_x >= x0 - W) & (row_x < x0 + tile_x + W)
        weight = jnp.where(inside, block[4:5] * live, 0.0)
        scale_full = jnp.broadcast_to(scale, (tile_x, lanes))
        start = -(W + block[1:2] * tile_y)
        start_full = jnp.broadcast_to(start, (tile_x, lanes))
        planes = []
        for j in range(ext_y):
            ty = (start_full + j) * scale_full
            planes.append(weight * jnp.exp2(exp_x - ty * ty))
        high, low = split(jnp.concatenate(planes, axis=0))
        return high, low, columns[:, 0:1], columns[:, 1:2]

    def accumulate(pair, carry):
        ah0, al0, s0, z0 = factors(2 * pair)
        ah1, al1, s1, z1 = factors(2 * pair + 1)
        plane = jnp.concatenate([ah0, ah1, al0, al1, ah0, ah1], axis=1)
        scale = jnp.concatenate([s0, s1], axis=0)
        centre = jnp.concatenate([z0, z1], axis=0)
        scale = jnp.broadcast_to(scale, (2 * lanes, ZTILE))
        centre = jnp.broadcast_to(centre, (2 * lanes, ZTILE))
        span = lax.broadcasted_iota(jnp.int32, (1, ZTILE), 1).astype(jnp.float32)
        for tile in range(depth // ZTILE):
            tz = ((span + tile * ZTILE) - centre) * scale
            zh, zl = split(jnp.exp2(-(tz * tz)))
            along_z = jnp.concatenate([zh, zh, zl], axis=0)
            out = jnp.dot(plane, along_z, preferred_element_type=jnp.float32)
            total[:, tile * ZTILE : (tile + 1) * ZTILE] += out
        return carry

    lax.fori_loop(0, lax.div(count + 1, 2), accumulate, 0)
    whole = total[...].reshape(ext_y, tile_x, depth)
    low_edge[...] = whole[:W]
    high_edge[...] = whole[ext_y - W :]
    core[...] = jnp.swapaxes(whole[W : ext_y - W], 0, 1)


def join_kernel(old_map, core, from_low, from_high, new_map):
    tile_y = core.shape[1]
    low = jnp.swapaxes(from_low[...], 0, 1)
    high = jnp.swapaxes(from_high[...], 0, 1)
    gap = jnp.zeros((core.shape[0], tile_y - 2 * W, core.shape[2]), jnp.float32)
    new_map[...] = old_map[...] + core[...] + jnp.concatenate([low, gap, high], axis=1)


def neighbours(rows, columns):
    row, column = lax.axis_index("gx"), lax.axis_index("gy")
    for step in (1, -1):
        yield 0, step, (column + step >= 0) & (column + step < columns)
    for step in (1, -1, 2, -2):
        yield step, 0, (row + step >= 0) & (row + step < rows)


def greet(links):
    row, column = lax.axis_index("gx"), lax.axis_index("gy")
    barrier = pltpu.get_barrier_semaphore()
    for dx, dy, there in links:

        @pl.when(there)
        def _():
            pl.semaphore_signal(barrier, 1, device_id=(row + dx, column + dy), device_id_type=MESH)

    pl.semaphore_wait(barrier, sum(there.astype(jnp.int32) for _, _, there in links))


def exchange_kernel(rows, columns, packed, blocks, own_sem, send_sem, recv_sem):
    row, column = lax.axis_index("gx"), lax.axis_index("gy")
    spans = {1: (1, 2, 6), -1: (0, 2, 1), 2: (2, 1, 8), -2: (0, 1, 0)}
    links = list(neighbours(rows, columns))
    for place, (dx, dy, there) in enumerate(links):

        @pl.when(jnp.logical_not(there))
        def _():
            if dx:
                first, number, group = spans[-dx]
                blocks[pl.ds(group, number)] = jnp.zeros((number,) + blocks.shape[1:], jnp.float32)
            else:
                blocks[pl.ds(3, 3), 1 - dy] = jnp.zeros((3,) + blocks.shape[2:], jnp.float32)

    greet(links)
    own = pltpu.make_async_copy(packed.at[1], blocks.at[pl.ds(3, 3), 1], own_sem)
    own.start()

    def copy(place):
        dx, dy, there = links[place]
        if dx:
            first, number, group = spans[dx]
            source, landing = blocks.at[pl.ds(3 + first, number)], blocks.at[pl.ds(group, number)]
        else:
            source, landing = packed.at[1 + dy], blocks.at[pl.ds(3, 3), 1 + dy]
        return pltpu.make_async_remote_copy(
            src_ref=source,
            dst_ref=landing,
            send_sem=send_sem.at[place],
            recv_sem=recv_sem.at[place],
            device_id=(row + dx, column + dy),
            device_id_type=MESH,
        )

    def arrived(place):
        dx, dy, _ = links[place]
        opposite = [there for x, y, there in links if (x, y) == (-dx, -dy)][0]

        @pl.when(opposite)
        def _():
            copy(place).wait_recv()

    def each(places, act):
        for place in places:

            @pl.when(links[place][2])
            def _():
                act(copy(place))

    each((0, 1), lambda c: c.start())
    own.wait()
    arrived(0)
    arrived(1)
    each((4, 5, 2, 3), lambda c: c.start())
    each((0, 1), lambda c: c.wait_send())
    for place in (2, 3, 4, 5):
        arrived(place)
    each((2, 3, 4, 5), lambda c: c.wait_send())


def edge_kernel(columns, low_edge, high_edge, from_low, from_high, send_sem, recv_sem):
    row, column = lax.axis_index("gx"), lax.axis_index("gy")
    links = [(0, 1, column + 1 < columns), (0, -1, column >= 1)]
    ends = [(high_edge, from_low), (low_edge, from_high)]
    for place, (_, _, there) in enumerate(links):

        @pl.when(jnp.logical_not(there))
        def _():
            landing = ends[1 - place][1]
            landing[...] = jnp.zeros_like(landing)

    greet(links)

    def copy(place):
        return pltpu.make_async_remote_copy(
            src_ref=ends[place][0],
            dst_ref=ends[place][1],
            send_sem=send_sem.at[place],
            recv_sem=recv_sem.at[place],
            device_id=(row, column + links[place][1]),
            device_id_type=MESH,
        )

    for place in (0, 1):

        @pl.when(links[place][2])
        def _():
            copy(place).start()

    for place in (0, 1):

        @pl.when(links[1 - place][2])
        def _():
            copy(place).wait_recv()

        @pl.when(links[place][2])
        def _():
            copy(place).wait_send()


def body(rows, columns, offsets, widths, solvation, heading, old_map):
    tile_x, tile_y, depth = old_map.shape
    lanes = offsets.shape[2]
    packed = pl.pallas_call(
        pack_kernel,
        out_shape=jax.ShapeDtypeStruct((9 * SLOTS, ROWS, lanes), jnp.float32),
        in_specs=[SMEM, VMEM, VMEM, VMEM],
        out_specs=VMEM,
        scratch_shapes=[pltpu.SMEM((9,), jnp.int32)],
    )(heading, offsets, widths, solvation)
    blocks = pl.pallas_call(
        functools.partial(exchange_kernel, rows, columns),
        out_shape=jax.ShapeDtypeStruct((len(HOMES), 3, SLOTS, ROWS, lanes), jnp.float32),
        in_specs=[VMEM],
        out_specs=VMEM,
        scratch_shapes=[
            pltpu.SemaphoreType.DMA,
            pltpu.SemaphoreType.DMA((6,)),
            pltpu.SemaphoreType.DMA((6,)),
        ],
        compiler_params=pltpu.CompilerParams(collective_id=0, has_side_effects=True),
    )(packed.reshape(3, 3, SLOTS, ROWS, lanes))
    blocks = blocks.reshape(-1, ROWS, lanes)
    number = blocks.shape[0]
    edge = jax.ShapeDtypeStruct((W, tile_x, depth), jnp.float32)
    core, low_edge, high_edge = pl.pallas_call(
        functools.partial(field_kernel, rows),
        out_shape=(jax.ShapeDtypeStruct(old_map.shape, jnp.float32), edge, edge),
        in_specs=[VMEM],
        out_specs=(VMEM, VMEM, VMEM),
        scratch_shapes=[
            pltpu.VMEM(((tile_y + 2 * W) * tile_x, depth), jnp.float32),
            pltpu.SMEM((number, lanes), jnp.float32),
            pltpu.SMEM((number + 2,), jnp.int32),
            pltpu.SMEM((number + 2,), jnp.int32),
            pltpu.SemaphoreType.DMA,
        ],
    )(blocks)
    from_low, from_high = pl.pallas_call(
        functools.partial(edge_kernel, columns),
        out_shape=(edge, edge),
        in_specs=[VMEM, VMEM],
        out_specs=(VMEM, VMEM),
        scratch_shapes=[pltpu.SemaphoreType.DMA((2,)), pltpu.SemaphoreType.DMA((2,))],
        compiler_params=pltpu.CompilerParams(collective_id=1, has_side_effects=True),
    )(low_edge, high_edge)
    return pl.pallas_call(
        join_kernel,
        out_shape=jax.ShapeDtypeStruct(old_map.shape, jnp.float32),
        in_specs=[VMEM] * 4,
        out_specs=VMEM,
    )(old_map, core, from_low, from_high)


def solution(mesh):
    placed = (
        P(("gx", "gy"), None, None),
        P(("gx", "gy"), None),
        P(("gx", "gy"), None),
        P(("gx", "gy"), None),
        P("gx", "gy", None),
    )
    return jax.shard_map(
        functools.partial(body, mesh.shape["gx"], mesh.shape["gy"]), mesh=mesh, in_specs=placed, out_specs=P("gx", "gy", None), check_vma=False
    )
```

```python
import functools
import math

import jax
import jax.numpy as jnp
from jax import lax
from jax.experimental import pallas as pl
from jax.experimental.pallas import tpu as pltpu
from jax.sharding import PartitionSpec as P

SLOTS = 3
W = 5
FEATURES = 5
ROWS = SLOTS * FEATURES + 1
HOMES = (1, 0, 1, -1, 0, 1, -1, 0, -1)
ZTILE = 256
MESH = pl.DeviceIdType.MESH
VMEM = pl.BlockSpec(memory_space=pltpu.VMEM)
SMEM = pl.BlockSpec(memory_space=pltpu.SMEM)


def pack_kernel(heading, offsets, widths, solvation, packed, taken):
    packed[...] = jnp.zeros_like(packed)
    for number in range(9):
        taken[number] = 0
    lanes = offsets.shape[2]
    for block in range(offsets.shape[0]):
        target = heading[block]
        group = lax.rem(target, 3) * 3 + lax.div(target, 3)
        rank = taken[group]
        taken[group] = rank + 1
        packed[group, pl.ds(rank * FEATURES, FEATURES)] = jnp.concatenate(
            [offsets[block], widths[pl.ds(block, 1)], solvation[pl.ds(block, 1)]], axis=0
        )
    for number in range(9):
        packed[number, ROWS - 1 :] = jnp.full((1, lanes), taken[number].astype(jnp.float32))


def split(value):
    high = value.astype(jnp.bfloat16)
    return high, (value - high.astype(jnp.float32)).astype(jnp.bfloat16)


def field_kernel(
    rows, blocks, core, low_edge, high_edge, total, filled, groups, starts, homes, sem
):
    tile_x, tile_y, depth = core.shape
    lanes = blocks.shape[2]
    ext_y = tile_y + 2 * W
    fetch = pltpu.make_async_copy(blocks.at[:, ROWS - 1], filled, sem)
    fetch.start()
    total[...] = jnp.zeros_like(total)
    fetch.wait()
    row = lax.axis_index("gx")
    count = jnp.int32(0)
    for group in range(blocks.shape[0]):
        home = HOMES[group // 3]
        within = (row + home >= 0) & (row + home < rows)
        number = jnp.where(within, filled[group, 0].astype(jnp.int32), 0)
        for rank in range(SLOTS):
            groups[count + rank] = group
            starts[count + rank] = rank * FEATURES
            homes[count + rank] = home
        count = count + number
    groups[count] = 0
    starts[count] = 0
    homes[count] = 0
    root = math.sqrt(0.5 * math.log2(math.e))
    row_x = lax.broadcasted_iota(jnp.int32, (tile_x, lanes), 0)

    def factors(number):
        live = jnp.where(number < count, 1.0, 0.0)
        block = blocks[groups[number], pl.ds(starts[number], FEATURES)]
        home = homes[number]
        width = jnp.where(number < count, block[3:4], 1.0)
        scale = root / width
        pz = block[2:3] * depth
        columns = jnp.concatenate([-scale * scale, pz, jnp.zeros((6, lanes), jnp.float32)], axis=0).T
        x0 = home * tile_x
        delta_x = (row_x - x0).astype(jnp.float32) - block[0:1] * tile_x
        tx = delta_x * scale
        exp_x = -(tx * tx)
        inside = (row_x >= x0 - W) & (row_x < x0 + tile_x + W)
        weight = jnp.where(inside, block[4:5] * live, 0.0)
        scale_full = jnp.broadcast_to(scale, (tile_x, lanes))
        start = -(W + block[1:2] * tile_y)
        start_full = jnp.broadcast_to(start, (tile_x, lanes))
        planes = []
        for j in range(ext_y):
            ty = (start_full + j) * scale_full
            planes.append(weight * jnp.exp2(exp_x - ty * ty))
        high, low = split(jnp.concatenate(planes, axis=0))
        return high, low, columns[:, 0:1], columns[:, 1:2]

    def accumulate(pair, carry):
        ah0, al0, s0, z0 = factors(2 * pair)
        ah1, al1, s1, z1 = factors(2 * pair + 1)
        plane = jnp.concatenate([ah0, ah1, al0, al1, ah0, ah1], axis=1)
        scale = jnp.concatenate([s0, s1], axis=0)
        centre = jnp.concatenate([z0, z1], axis=0)
        scale = jnp.broadcast_to(scale, (2 * lanes, ZTILE))
        centre = jnp.broadcast_to(centre, (2 * lanes, ZTILE))
        span = lax.broadcasted_iota(jnp.int32, (1, ZTILE), 1).astype(jnp.float32)
        for tile in range(depth // ZTILE):
            delta_z = (span + tile * ZTILE) - centre
            zh, zl = split(jnp.exp2(delta_z * delta_z * scale))
            along_z = jnp.concatenate([zh, zh, zl], axis=0)
            out = jnp.dot(plane, along_z, preferred_element_type=jnp.float32)
            total[:, tile * ZTILE : (tile + 1) * ZTILE] += out
        return carry

    lax.fori_loop(0, lax.div(count + 1, 2), accumulate, 0)
    whole = total[...].reshape(ext_y, tile_x, depth)
    low_edge[...] = whole[:W]
    high_edge[...] = whole[ext_y - W :]
    core[...] = jnp.swapaxes(whole[W : ext_y - W], 0, 1)


def join_kernel(old_map, core, from_low, from_high, new_map):
    tile_y = core.shape[1]
    low = jnp.swapaxes(from_low[...], 0, 1)
    high = jnp.swapaxes(from_high[...], 0, 1)
    gap = jnp.zeros((core.shape[0], tile_y - 2 * W, core.shape[2]), jnp.float32)
    new_map[...] = old_map[...] + core[...] + jnp.concatenate([low, gap, high], axis=1)


def neighbours(rows, columns):
    row, column = lax.axis_index("gx"), lax.axis_index("gy")
    for step in (1, -1):
        yield 0, step, (column + step >= 0) & (column + step < columns)
    for step in (1, -1, 2, -2):
        yield step, 0, (row + step >= 0) & (row + step < rows)


def greet(links):
    row, column = lax.axis_index("gx"), lax.axis_index("gy")
    barrier = pltpu.get_barrier_semaphore()
    for dx, dy, there in links:

        @pl.when(there)
        def _():
            pl.semaphore_signal(barrier, 1, device_id=(row + dx, column + dy), device_id_type=MESH)

    pl.semaphore_wait(barrier, sum(there.astype(jnp.int32) for _, _, there in links))


def exchange_kernel(rows, columns, packed, blocks, own_sem, send_sem, recv_sem):
    row, column = lax.axis_index("gx"), lax.axis_index("gy")
    spans = {1: (1, 2, 6), -1: (0, 2, 1), 2: (2, 1, 8), -2: (0, 1, 0)}
    links = list(neighbours(rows, columns))
    for place, (dx, dy, there) in enumerate(links):

        @pl.when(jnp.logical_not(there))
        def _():
            if dx:
                first, number, group = spans[-dx]
                blocks[pl.ds(group, number)] = jnp.zeros((number,) + blocks.shape[1:], jnp.float32)
            else:
                blocks[pl.ds(3, 3), 1 - dy] = jnp.zeros((3,) + blocks.shape[2:], jnp.float32)

    greet(links)
    own = pltpu.make_async_copy(packed.at[1], blocks.at[pl.ds(3, 3), 1], own_sem)
    own.start()

    def copy(place):
        dx, dy, there = links[place]
        if dx:
            first, number, group = spans[dx]
            source, landing = blocks.at[pl.ds(3 + first, number)], blocks.at[pl.ds(group, number)]
        else:
            source, landing = packed.at[1 + dy], blocks.at[pl.ds(3, 3), 1 + dy]
        return pltpu.make_async_remote_copy(
            src_ref=source,
            dst_ref=landing,
            send_sem=send_sem.at[place],
            recv_sem=recv_sem.at[place],
            device_id=(row + dx, column + dy),
            device_id_type=MESH,
        )

    def arrived(place):
        dx, dy, _ = links[place]
        opposite = [there for x, y, there in links if (x, y) == (-dx, -dy)][0]

        @pl.when(opposite)
        def _():
            copy(place).wait_recv()

    def each(places, act):
        for place in places:

            @pl.when(links[place][2])
            def _():
                act(copy(place))

    each((0, 1), lambda c: c.start())
    own.wait()
    arrived(0)
    arrived(1)
    each((4, 5, 2, 3), lambda c: c.start())
    each((0, 1), lambda c: c.wait_send())
    for place in (2, 3, 4, 5):
        arrived(place)
    each((2, 3, 4, 5), lambda c: c.wait_send())


def edge_kernel(columns, low_edge, high_edge, from_low, from_high, send_sem, recv_sem):
    row, column = lax.axis_index("gx"), lax.axis_index("gy")
    links = [(0, 1, column + 1 < columns), (0, -1, column >= 1)]
    ends = [(high_edge, from_low), (low_edge, from_high)]
    for place, (_, _, there) in enumerate(links):

        @pl.when(jnp.logical_not(there))
        def _():
            landing = ends[1 - place][1]
            landing[...] = jnp.zeros_like(landing)

    greet(links)

    def copy(place):
        return pltpu.make_async_remote_copy(
            src_ref=ends[place][0],
            dst_ref=ends[place][1],
            send_sem=send_sem.at[place],
            recv_sem=recv_sem.at[place],
            device_id=(row, column + links[place][1]),
            device_id_type=MESH,
        )

    for place in (0, 1):

        @pl.when(links[place][2])
        def _():
            copy(place).start()

    for place in (0, 1):

        @pl.when(links[1 - place][2])
        def _():
            copy(place).wait_recv()

        @pl.when(links[place][2])
        def _():
            copy(place).wait_send()


def body(rows, columns, offsets, widths, solvation, heading, old_map):
    tile_x, tile_y, depth = old_map.shape
    lanes = offsets.shape[2]
    packed = pl.pallas_call(
        pack_kernel,
        out_shape=jax.ShapeDtypeStruct((9, ROWS, lanes), jnp.float32),
        in_specs=[SMEM, VMEM, VMEM, VMEM],
        out_specs=VMEM,
        scratch_shapes=[pltpu.SMEM((9,), jnp.int32)],
    )(heading[:, 0], offsets, widths, solvation)
    blocks = pl.pallas_call(
        functools.partial(exchange_kernel, rows, columns),
        out_shape=jax.ShapeDtypeStruct((len(HOMES), 3, ROWS, lanes), jnp.float32),
        in_specs=[VMEM],
        out_specs=VMEM,
        scratch_shapes=[
            pltpu.SemaphoreType.DMA,
            pltpu.SemaphoreType.DMA((6,)),
            pltpu.SemaphoreType.DMA((6,)),
        ],
        compiler_params=pltpu.CompilerParams(collective_id=0, has_side_effects=True),
    )(packed.reshape(3, 3, ROWS, lanes))
    blocks = blocks.reshape(-1, ROWS, lanes)
    number = blocks.shape[0]
    edge = jax.ShapeDtypeStruct((W, tile_x, depth), jnp.float32)
    core, low_edge, high_edge = pl.pallas_call(
        functools.partial(field_kernel, rows),
        out_shape=(jax.ShapeDtypeStruct(old_map.shape, jnp.float32), edge, edge),
        in_specs=[VMEM],
        out_specs=(VMEM, VMEM, VMEM),
        scratch_shapes=[
            pltpu.VMEM(((tile_y + 2 * W) * tile_x, depth), jnp.float32),
            pltpu.SMEM((number, lanes), jnp.float32),
            pltpu.SMEM((number * SLOTS + SLOTS,), jnp.int32),
            pltpu.SMEM((number * SLOTS + SLOTS,), jnp.int32),
            pltpu.SMEM((number * SLOTS + SLOTS,), jnp.int32),
            pltpu.SemaphoreType.DMA,
        ],
    )(blocks)
    from_low, from_high = pl.pallas_call(
        functools.partial(edge_kernel, columns),
        out_shape=(edge, edge),
        in_specs=[VMEM, VMEM],
        out_specs=(VMEM, VMEM),
        scratch_shapes=[pltpu.SemaphoreType.DMA((2,)), pltpu.SemaphoreType.DMA((2,))],
        compiler_params=pltpu.CompilerParams(collective_id=1, has_side_effects=True),
    )(low_edge, high_edge)
    return pl.pallas_call(
        join_kernel,
        out_shape=jax.ShapeDtypeStruct(old_map.shape, jnp.float32),
        in_specs=[VMEM] * 4,
        out_specs=VMEM,
    )(old_map, core, from_low, from_high)


def solution(mesh):
    placed = (
        P(("gx", "gy"), None, None),
        P(("gx", "gy"), None),
        P(("gx", "gy"), None),
        P(("gx", "gy"), None),
        P("gx", "gy", None),
    )
    return jax.shard_map(
        functools.partial(body, mesh.shape["gx"], mesh.shape["gy"]), mesh=mesh, in_specs=placed, out_specs=P("gx", "gy", None), check_vma=False
    )
```

```python
import functools
import math

import jax
import jax.numpy as jnp
from jax import lax
from jax.experimental import pallas as pl
from jax.experimental.pallas import tpu as pltpu
from jax.sharding import PartitionSpec as P

SLOTS = 3
W = 5
FEATURES = 5
ROWS = SLOTS * FEATURES + 1
HOMES = (1, 0, 1, -1, 0, 1, -1, 0, -1)
ZTILE = 256
MESH = pl.DeviceIdType.MESH
VMEM = pl.BlockSpec(memory_space=pltpu.VMEM)
SMEM = pl.BlockSpec(memory_space=pltpu.SMEM)


def pack_kernel(heading, offsets, widths, solvation, packed, taken):
    packed[...] = jnp.zeros_like(packed)
    for number in range(9):
        taken[number] = 0
    lanes = offsets.shape[2]
    for block in range(offsets.shape[0]):
        target = heading[block]
        group = lax.rem(target, 3) * 3 + lax.div(target, 3)
        rank = taken[group]
        taken[group] = rank + 1
        packed[group, pl.ds(rank * FEATURES, FEATURES)] = jnp.concatenate(
            [offsets[block], widths[pl.ds(block, 1)], solvation[pl.ds(block, 1)]], axis=0
        )
    for number in range(9):
        packed[number, ROWS - 1 :] = jnp.full((1, lanes), taken[number].astype(jnp.float32))


def split(value):
    high = value.astype(jnp.bfloat16)
    return high, (value - high.astype(jnp.float32)).astype(jnp.bfloat16)


def field_kernel(
    rows, blocks, core, low_edge, high_edge, total, filled, groups, starts, homes, sem
):
    tile_x, tile_y, depth = core.shape
    lanes = blocks.shape[2]
    ext_y = tile_y + 2 * W
    fetch = pltpu.make_async_copy(blocks.at[:, ROWS - 1], filled, sem)
    fetch.start()
    total[...] = jnp.zeros_like(total)
    fetch.wait()
    row = lax.axis_index("gx")
    count = jnp.int32(0)
    for group in range(blocks.shape[0]):
        home = HOMES[group // 3]
        within = (row + home >= 0) & (row + home < rows)
        number = jnp.where(within, filled[group, 0].astype(jnp.int32), 0)
        for rank in range(SLOTS):
            groups[count + rank] = group
            starts[count + rank] = rank * FEATURES
            homes[count + rank] = home
        count = count + number
    groups[count] = 0
    starts[count] = 0
    homes[count] = 0
    root = math.sqrt(0.5 * math.log2(math.e))
    row_x = lax.broadcasted_iota(jnp.int32, (tile_x, lanes), 0)

    def factors(number):
        live = jnp.where(number < count, 1.0, 0.0)
        block = blocks[groups[number], pl.ds(starts[number], FEATURES)]
        home = homes[number]
        width = jnp.where(number < count, block[3:4], 1.0)
        scale = root / width
        pz = block[2:3] * depth
        columns = jnp.concatenate([-scale * scale, pz, jnp.zeros((6, lanes), jnp.float32)], axis=0).T
        x0 = home * tile_x
        delta_x = (row_x - x0).astype(jnp.float32) - block[0:1] * tile_x
        tx = delta_x * scale
        exp_x = -(tx * tx)
        inside = (row_x >= x0 - W) & (row_x < x0 + tile_x + W)
        weight = jnp.where(inside, block[4:5] * live, 0.0)
        scale_full = jnp.broadcast_to(scale, (tile_x, lanes))
        start = -(W + block[1:2] * tile_y)
        start_full = jnp.broadcast_to(start, (tile_x, lanes))
        planes = []
        for j in range(ext_y):
            ty = (start_full + j) * scale_full
            planes.append(weight * jnp.exp2(exp_x - ty * ty))
        high, low = split(jnp.concatenate(planes, axis=0))
        return high, low, columns[:, 0:1], columns[:, 1:2]

    def accumulate(pair, carry):
        ah0, al0, s0, z0 = factors(2 * pair)
        ah1, al1, s1, z1 = factors(2 * pair + 1)
        plane = jnp.concatenate([ah0, ah1, al0, al1, ah0, ah1], axis=1)
        scale = jnp.concatenate([s0, s1], axis=0)
        centre = jnp.concatenate([z0, z1], axis=0)
        scale = jnp.broadcast_to(scale, (2 * lanes, ZTILE))
        centre = jnp.broadcast_to(centre, (2 * lanes, ZTILE))
        span = lax.broadcasted_iota(jnp.int32, (1, ZTILE), 1).astype(jnp.float32)
        for tile in range(depth // ZTILE):
            delta_z = (span + tile * ZTILE) - centre
            zh, zl = split(jnp.exp2(delta_z * delta_z * scale))
            along_z = jnp.concatenate([zh, zh, zl], axis=0)
            out = jnp.dot(plane, along_z, preferred_element_type=jnp.float32)
            total[:, tile * ZTILE : (tile + 1) * ZTILE] += out
        return carry

    lax.fori_loop(0, lax.div(count + 1, 2), accumulate, 0)
    whole = total[...].reshape(ext_y, tile_x, depth)
    low_edge[...] = whole[:W]
    high_edge[...] = whole[ext_y - W :]
    core[...] = jnp.swapaxes(whole[W : ext_y - W], 0, 1)


def neighbours(rows, columns):
    row, column = lax.axis_index("gx"), lax.axis_index("gy")
    for step in (1, -1):
        yield 0, step, (column + step >= 0) & (column + step < columns)
    for step in (1, -1, 2, -2):
        yield step, 0, (row + step >= 0) & (row + step < rows)


def greet(links):
    row, column = lax.axis_index("gx"), lax.axis_index("gy")
    barrier = pltpu.get_barrier_semaphore()
    for dx, dy, there in links:

        @pl.when(there)
        def _():
            pl.semaphore_signal(barrier, 1, device_id=(row + dx, column + dy), device_id_type=MESH)

    pl.semaphore_wait(barrier, sum(there.astype(jnp.int32) for _, _, there in links))


def exchange_kernel(rows, columns, packed, blocks, own_sem, send_sem, recv_sem):
    row, column = lax.axis_index("gx"), lax.axis_index("gy")
    spans = {1: (1, 2, 6), -1: (0, 2, 1), 2: (2, 1, 8), -2: (0, 1, 0)}
    links = list(neighbours(rows, columns))
    for place, (dx, dy, there) in enumerate(links):

        @pl.when(jnp.logical_not(there))
        def _():
            if dx:
                first, number, group = spans[-dx]
                blocks[pl.ds(group, number)] = jnp.zeros((number,) + blocks.shape[1:], jnp.float32)
            else:
                blocks[pl.ds(3, 3), 1 - dy] = jnp.zeros((3,) + blocks.shape[2:], jnp.float32)

    greet(links)
    own = pltpu.make_async_copy(packed.at[1], blocks.at[pl.ds(3, 3), 1], own_sem)
    own.start()

    def copy(place):
        dx, dy, there = links[place]
        if dx:
            first, number, group = spans[dx]
            source, landing = blocks.at[pl.ds(3 + first, number)], blocks.at[pl.ds(group, number)]
        else:
            source, landing = packed.at[1 + dy], blocks.at[pl.ds(3, 3), 1 + dy]
        return pltpu.make_async_remote_copy(
            src_ref=source,
            dst_ref=landing,
            send_sem=send_sem.at[place],
            recv_sem=recv_sem.at[place],
            device_id=(row + dx, column + dy),
            device_id_type=MESH,
        )

    def arrived(place):
        dx, dy, _ = links[place]
        opposite = [there for x, y, there in links if (x, y) == (-dx, -dy)][0]

        @pl.when(opposite)
        def _():
            copy(place).wait_recv()

    def each(places, act):
        for place in places:

            @pl.when(links[place][2])
            def _():
                act(copy(place))

    each((0, 1), lambda c: c.start())
    own.wait()
    arrived(0)
    arrived(1)
    each((4, 5, 2, 3), lambda c: c.start())
    each((0, 1), lambda c: c.wait_send())
    for place in (2, 3, 4, 5):
        arrived(place)
    each((2, 3, 4, 5), lambda c: c.wait_send())


def edge_kernel(
    columns, low_edge, high_edge, old_map, core, new_map, from_low, from_high, send_sem, recv_sem
):
    tile_y = core.shape[1]
    row, column = lax.axis_index("gx"), lax.axis_index("gy")
    links = [(0, 1, column + 1 < columns), (0, -1, column >= 1)]
    ends = [(high_edge, from_low), (low_edge, from_high)]
    greet(links)

    def copy(place):
        return pltpu.make_async_remote_copy(
            src_ref=ends[place][0],
            dst_ref=ends[place][1],
            send_sem=send_sem.at[place],
            recv_sem=recv_sem.at[place],
            device_id=(row, column + links[place][1]),
            device_id_type=MESH,
        )

    for place in (0, 1):

        @pl.when(links[place][2])
        def _():
            copy(place).start()

    new_map[...] = old_map[...] + core[...]
    for place in (0, 1):

        @pl.when(links[1 - place][2])
        def _():
            copy(place).wait_recv()
            first = 0 if place == 0 else tile_y - W
            new_map[:, first : first + W] += jnp.swapaxes(ends[place][1][...], 0, 1)

        @pl.when(links[place][2])
        def _():
            copy(place).wait_send()


def body(rows, columns, offsets, widths, solvation, heading, old_map):
    tile_x, tile_y, depth = old_map.shape
    lanes = offsets.shape[2]
    packed = pl.pallas_call(
        pack_kernel,
        out_shape=jax.ShapeDtypeStruct((9, ROWS, lanes), jnp.float32),
        in_specs=[SMEM, VMEM, VMEM, VMEM],
        out_specs=VMEM,
        scratch_shapes=[pltpu.SMEM((9,), jnp.int32)],
    )(heading[:, 0], offsets, widths, solvation)
    blocks = pl.pallas_call(
        functools.partial(exchange_kernel, rows, columns),
        out_shape=jax.ShapeDtypeStruct((len(HOMES), 3, ROWS, lanes), jnp.float32),
        in_specs=[VMEM],
        out_specs=VMEM,
        scratch_shapes=[
            pltpu.SemaphoreType.DMA,
            pltpu.SemaphoreType.DMA((6,)),
            pltpu.SemaphoreType.DMA((6,)),
        ],
        compiler_params=pltpu.CompilerParams(collective_id=0, has_side_effects=True),
    )(packed.reshape(3, 3, ROWS, lanes))
    blocks = blocks.reshape(-1, ROWS, lanes)
    number = blocks.shape[0]
    edge = jax.ShapeDtypeStruct((W, tile_x, depth), jnp.float32)
    core, low_edge, high_edge = pl.pallas_call(
        functools.partial(field_kernel, rows),
        out_shape=(jax.ShapeDtypeStruct(old_map.shape, jnp.float32), edge, edge),
        in_specs=[VMEM],
        out_specs=(VMEM, VMEM, VMEM),
        scratch_shapes=[
            pltpu.VMEM(((tile_y + 2 * W) * tile_x, depth), jnp.float32),
            pltpu.SMEM((number, lanes), jnp.float32),
            pltpu.SMEM((number * SLOTS + SLOTS,), jnp.int32),
            pltpu.SMEM((number * SLOTS + SLOTS,), jnp.int32),
            pltpu.SMEM((number * SLOTS + SLOTS,), jnp.int32),
            pltpu.SemaphoreType.DMA,
        ],
    )(blocks)
    return pl.pallas_call(
        functools.partial(edge_kernel, columns),
        out_shape=jax.ShapeDtypeStruct(old_map.shape, jnp.float32),
        in_specs=[VMEM] * 4,
        out_specs=VMEM,
        scratch_shapes=[
            pltpu.VMEM((W, tile_x, depth), jnp.float32),
            pltpu.VMEM((W, tile_x, depth), jnp.float32),
            pltpu.SemaphoreType.DMA((2,)),
            pltpu.SemaphoreType.DMA((2,)),
        ],
        compiler_params=pltpu.CompilerParams(collective_id=1, has_side_effects=True),
    )(low_edge, high_edge, old_map, core)


def solution(mesh):
    placed = (
        P(("gx", "gy"), None, None),
        P(("gx", "gy"), None),
        P(("gx", "gy"), None),
        P(("gx", "gy"), None),
        P("gx", "gy", None),
    )
    return jax.shard_map(
        functools.partial(body, mesh.shape["gx"], mesh.shape["gy"]), mesh=mesh, in_specs=placed, out_specs=P("gx", "gy", None), check_vma=False
    )
```
